512 devices in a mesh: tm: 32 (over x_hi, z), cam: 16 (over x_lo, y, core).
Axes of the slice: x: 4 (x_hi: 2, x_lo: 2; x = x_hi * 2 + x_lo), y: 4, z: 16, core: 2. Of those that a mesh axis runs over, the one named last changes fastest.
Arguments:
- features: bfloat16 [16, 32, 64, 16, 128], P('cam', None, 'tm'), may hold values from -60 to 60
- disparity_base: int32 [1], replicated, may hold values from 0 to 3
- conv_one: float32 [4, 3, 3, 3], replicated, may hold values from -1.25 to 1.25
- conv_bias: float32 [4], replicated, may hold values from -4 to 4
- conv_two: float32 [4, 3, 3, 3], replicated, may hold values from -0.625 to 0.625
Outputs:
- disparity: float32 [16, 64, 16, 128], P('cam', 'tm')
The draws below stay inside these ranges and needn't reach their ends.
All inputs are finite; a program needn't handle non-finite values.
Results may differ from the reference program's by a relative error of at most 0.0003.
Values may be sent and summed in bfloat16 or wider, within the bound.
No kernel may reach another device: no remote copies, remote signals or barrier semaphores. Data moves between devices by JAX's collectives and lax.ppermute only.
A program may use at most 64 MiB of HBM per device.

```python
import math
import jax
import jax.numpy as jnp
from jax import lax

C = 32
NDISP = 32
HID = 4
RIG_COLS = 4
H = 16
W = 128
CAMS = 16
TFRAMES = 64


def draw_features(key, part):
    shape = (CAMS, C, TFRAMES, H, W)
    values = jax.random.normal(key, shape, jnp.float32)
    return jnp.clip(values, -60.0, 60.0).astype(jnp.bfloat16)


def scatter_about(key, extent, scale, bound, kind=jnp.bfloat16):
    result = scale * jax.random.normal(key, extent, jnp.float32)
    return jnp.clip(result, min=-bound, max=bound).astype(kind)


def setup_inputs(seed: int = 0) -> dict:
    streams_of = jax.random.split(jax.random.key(seed), 6)
    features = draw_features(jax.random.fold_in(streams_of[5], 71), 0)
    disparity_base = jax.random.randint(streams_of[1], (1,), 0, 4).astype(jnp.int32)
    conv_one = scatter_about(streams_of[2], (HID, 3, 3, 3), 27 ** -0.5, 1.25, jnp.float32)
    conv_bias = scatter_about(streams_of[3], (HID,), 1.0, 4.0, jnp.float32)
    conv_two = scatter_about(streams_of[4], (HID, 3, 3, 3), (27 * HID) ** -0.5, 0.625, jnp.float32)
    return dict(features=features, disparity_base=disparity_base, conv_one=conv_one, conv_bias=conv_bias, conv_two=conv_two)


group_width = 4

def correlate(own_features, partner_feat, lowest, dim, sign):
    margin = NDISP + 4
    widths = [(0, 0), (0, 0), (0, 0), (0, 0)]
    widths[dim] = (margin, margin)
    padded = jnp.pad(partner_feat, tuple(widths))
    length = own_features.shape[dim]
    factor = 1.0 / math.sqrt(own_features.shape[0])

    def single(level):
        anchor = (margin + sign * (lowest + level)).astype(jnp.int32)
        window = lax.dynamic_slice_in_dim(padded, anchor, length, dim)
        return jnp.einsum('cthw,cthw->thw', own_features, window, preferred_element_type=jnp.float32) * factor

    def groups(base):
        return jax.vmap(single)(base + jnp.arange(group_width, dtype=jnp.int32))
    group_starts = jnp.arange(0, NDISP, group_width, dtype=jnp.int32)
    summed = lax.map(groups, group_starts)
    return summed.reshape((NDISP,) + own_features.shape[1:])

def first_conv(extended, conv_one, conv_bias):
    frames = extended.shape[1] - 2
    height, width_cells = (extended.shape[2], extended.shape[3])
    padded = jnp.pad(extended, ((0, 0), (0, 0), (1, 1), (1, 1)))
    summed = jnp.zeros((conv_one.shape[0], extended.shape[0], frames, height, width_cells), jnp.float32)
    for time_lag in range(3):
        for height_lag in range(3):
            for width_lag in range(3):
                window = padded[:, time_lag:time_lag + frames, height_lag:height_lag + height, width_lag:width_lag + width_cells]
                summed = summed + conv_one[:, time_lag, height_lag, width_lag][:, None, None, None, None] * window[None]
    return jnp.maximum(summed + conv_bias[:, None, None, None, None], 0.0)

def second_conv(extended, conv_two):
    frames = extended.shape[2] - 2
    height, width_cells = (extended.shape[3], extended.shape[4])
    padded = jnp.pad(extended, ((0, 0), (0, 0), (0, 0), (1, 1), (1, 1)))
    summed = jnp.zeros((extended.shape[1], frames, height, width_cells), jnp.float32)
    for time_lag in range(3):
        for height_lag in range(3):
            for width_lag in range(3):
                window = padded[:, :, time_lag:time_lag + frames, height_lag:height_lag + height, width_lag:width_lag + width_cells]
                summed = summed + lax.optimization_barrier(jnp.sum(conv_two[:, time_lag, height_lag, width_lag][:, None, None, None, None] * window, axis=0))
    return summed

def expected_disparity(aggregated, lowest):
    largest = lax.optimization_barrier(jnp.max(aggregated, axis=0, keepdims=True))
    weights = jnp.exp(aggregated - largest)
    levels = (lowest + jnp.arange(NDISP, dtype=jnp.int32)).astype(jnp.float32)
    return lax.optimization_barrier(jnp.sum(weights * levels[:, None, None, None], axis=0)) / lax.optimization_barrier(jnp.sum(weights, axis=0))

def reference(features, disparity_base, conv_one, conv_bias, conv_two):
    cameras = features.shape[0]
    row_step = cameras // RIG_COLS
    lowest = disparity_base[0]

    def camera_disparity(camera):
        own_features = features[camera]

        def partner(offset, dim, sign):
            partner_feat = features[jnp.mod(camera + offset, cameras).astype(jnp.int32)]
            return correlate(own_features, partner_feat, lowest, dim, sign)
        summed = partner(1, 3, -1) + partner(-1, 3, 1)
        summed = summed + partner(row_step, 2, -1) + partner(-row_step, 2, 1)
        cost = summed / 4.0
        extended = jnp.pad(cost, ((0, 0), (1, 1), (0, 0), (0, 0)))
        hidden = first_conv(extended, conv_one, conv_bias)
        widened = jnp.pad(hidden, ((0, 0), (0, 0), (1, 1), (0, 0), (0, 0)))
        aggregated = cost + second_conv(widened, conv_two)
        return expected_disparity(aggregated, lowest)
    return lax.map(camera_disparity, jnp.arange(cameras, dtype=jnp.int32))
```

```python
import math

import jax
import jax.numpy as jnp
from jax import lax
from jax.experimental import pallas as pl
from jax.experimental.pallas import tpu as pltpu
from jax.sharding import PartitionSpec as P

NDISP = 32
HALF = NDISP // 2
RIG_COLS = 4
HID = 4
C = 32
T = 2
H = 16
W = 128
ROWS = T * H
PITCH = ROWS + 1
GROUP = 4
LEVELS = 2
FACTOR = 1.0 / math.sqrt(C) / 4.0
F32 = jnp.float32
BF16 = jnp.bfloat16
VMEM = pl.BlockSpec(memory_space=pltpu.VMEM)
SMEM = pl.BlockSpec(memory_space=pltpu.SMEM)


def passed_along(block, axis, distance):
    count = lax.axis_size(axis)
    return lax.ppermute(block, axis, [((i - distance) % count, i) for i in range(count)])


def shifted_along(block, axis, distance):
    count = lax.axis_size(axis)
    route = [(i, i + distance) for i in range(count) if 0 <= i + distance < count]
    return lax.ppermute(block, axis, route)


def two_parts(x):
    first = x.astype(BF16)
    return first, (x - first.astype(F32)).astype(BF16)


def across_kernel(base_ref, own_ref, right_ref, left_ref, high_ref, low_ref,
                  own_s, right_s, left_s, gram_0, gram_1, horiz_s):
    base = base_ref[0]
    grams = (gram_0, gram_1)

    def widen(i, carry):
        for k in range(4):
            c = i * 4 + k
            for source, target in ((own_ref, own_s), (right_ref, right_s), (left_ref, left_s)):
                target[pl.ds(c * PITCH, ROWS), :] = source[c].reshape(ROWS, W).astype(F32)
        return carry

    lax.fori_loop(0, C // 4, widen, 0)

    row = lax.broadcasted_iota(jnp.int32, (W, W), 0)
    col = lax.broadcasted_iota(jnp.int32, (W, W), 1)
    flip = (row + col == W - 1).astype(BF16)
    same = (row == col).astype(BF16)
    lane = lax.broadcasted_iota(jnp.int32, (8, W), 1)
    sub = lax.broadcasted_iota(jnp.int32, (8, W), 0)
    nt = (((1,), (1,)), ((), ()))

    def products(g):
        def stack(source):
            return [
                source[pl.ds(g * GROUP + i, C, stride=PITCH), :].astype(BF16) for i in range(GROUP)
            ]

        rights = lax.dot_general(flip, jnp.concatenate(stack(right_s), axis=0), nt,
                                 preferred_element_type=F32).astype(BF16)
        lefts = lax.dot_general(same, jnp.concatenate(stack(left_s), axis=0), nt,
                                preferred_element_type=F32).astype(BF16)
        mine = stack(own_s)
        blank = jnp.zeros((C, W), BF16)
        blocks = jnp.concatenate(
            [
                jnp.concatenate([mine[i] if i == k else blank for k in range(GROUP)], axis=1)
                for i in range(GROUP)
            ],
            axis=0,
        )
        gram = grams[g % 2]
        gram[0:W, :] = jnp.dot(rights, blocks, preferred_element_type=F32)
        gram[W : 2 * W, :] = jnp.dot(lefts, blocks, preferred_element_type=F32)

    def diagonals(offset, read):
        low = offset & 7
        index = (sub + low) & 7
        stay = sub + low < 8
        tiles = [read(i) for i in range(W // 8)] + [jnp.zeros((8, W), F32)] * 4
        for bit, count in ((6, 12), (5, 8), (4, 6), (3, 5)):
            step = 1 << (bit - 3)
            take = (offset & (1 << bit)) != 0
            tiles = [jnp.where(take, tiles[i + step], tiles[i]) for i in range(count)]
        turned = [jnp.take_along_axis(tile, index, axis=0, mode="promise_in_bounds") for tile in tiles]
        inside = offset < W
        return [
            jnp.where(inside, jnp.where(stay, turned[i], turned[i + 1]), 0.0)
            for i in range(NDISP // 8)
        ]

    def shift(g):
        gram = grams[g % 2]
        for i in range(GROUP):
            from_right = diagonals(
                W - 1 - lane + base, lambda k: gram[8 * k : 8 * k + 8, i * W : (i + 1) * W])
            from_left = diagonals(
                lane + base, lambda k: gram[W + 8 * k : W + 8 * k + 8, i * W : (i + 1) * W])
            for k in range(NDISP // 8):
                horiz_s[pl.ds((g * GROUP + i) * PITCH + 8 * k, 8), :] = from_right[k] + from_left[k]

    groups = ROWS // GROUP
    products(0)
    for g in range(groups):
        if g + 1 < groups:
            products(g + 1)
        shift(g)

    for level in range(NDISP):
        summed = horiz_s[pl.ds(level, ROWS, stride=PITCH), :] * FACTOR
        if level < HALF:
            low_ref[level] = summed
        else:
            high_ref[level - HALF] = summed


def across(base, own, right, left):
    flat = pltpu.VMEM((C * PITCH, W), F32)
    gram = pltpu.VMEM((2 * W, GROUP * W), F32)
    half = jax.ShapeDtypeStruct((HALF, ROWS, W), F32)
    return pl.pallas_call(
        across_kernel,
        out_shape=(half, half),
        in_specs=[SMEM, VMEM, VMEM, VMEM],
        out_specs=(VMEM, VMEM),
        scratch_shapes=[flat, flat, flat, gram, gram, flat],
        compiler_params=pltpu.CompilerParams(vmem_limit_bytes=16 << 20),
        cost_estimate=pl.CostEstimate(flops=2 << 30, bytes_accessed=2 << 20, transcendentals=0),
        name="across",
    )(base, own, right, left)


def along_kernel(base_ref, low_ref, own_ref, down_ref, up_ref, cost_ref, down_s, up_s, vert_s):
    base = base_ref[0]
    half = H // 2
    zeros = jnp.zeros((H, W), F32)
    for target in (down_s, up_s):
        target[0:H, :] = zeros

    def widen(i, carry):
        for k in range(2):
            c = i * 2 + k
            for source, target in ((down_ref, down_s), (up_ref, up_s)):
                for t in range(T):
                    start = (c * T + t) * 2 * H + H
                    target[pl.ds(start, H), :] = source[c, t].astype(F32)
                    target[pl.ds(start + H, H), :] = zeros
        return carry

    lax.fori_loop(0, C // 2, widen, 0)

    for t in range(T):

        def channels(i, sums, t=t):
            for k in range(4):
                c = i * 4 + k
                mine = own_ref[c, t].astype(F32)
                mine_low, mine_high = mine[:half], mine[half:]
                start = (c * T + t) * 2 * H + H
                results = []
                for level in range(H):
                    low, high = sums[2 * level], sums[2 * level + 1]
                    part_low = up_s[pl.ds(start + level, half), :]
                    part_high = down_s[pl.ds(start + half - level, half), :]
                    if level < half:
                        part_low = part_low + down_s[pl.ds(start - level, half), :]
                        part_high = part_high + up_s[pl.ds(start + half + level, half), :]
                    results += [low + mine_low * part_low, high + mine_high * part_high]
                sums = tuple(results)
            return sums

        sums = lax.fori_loop(0, C // 4, channels,
                             tuple(jnp.zeros((half, W), F32) for _ in range(2 * H)))
        for level in range(H):
            vert_s[level, t * H : t * H + half, :] = sums[2 * level]
            vert_s[level, t * H + half : (t + 1) * H, :] = sums[2 * level + 1]
    for level in range(H, H + 4):
        vert_s[level] = jnp.zeros((ROWS, W), F32)
    for level in range(HALF):
        cost_ref[level] = low_ref[level] + vert_s[base + level] * FACTOR


def along(base, low, own, down, up):
    padded = pltpu.VMEM((C * T * 2 * H + H, W), F32)
    return pl.pallas_call(
        along_kernel,
        out_shape=jax.ShapeDtypeStruct((HALF, ROWS, W), F32),
        in_specs=[SMEM] + [VMEM] * 4,
        out_specs=VMEM,
        scratch_shapes=[padded, padded, pltpu.VMEM((H + 4, ROWS, W), F32)],
        compiler_params=pltpu.CompilerParams(vmem_limit_bytes=12 << 20),
        cost_estimate=pl.CostEstimate(flops=2 << 30, bytes_accessed=2 << 20, transcendentals=0),
        name="along",
    )(base, low, own, down, up)


def prepare_kernel(keep_ref, one_in, bias_in, two_in, one_ref, bias_ref, two_ref):
    sub = lax.broadcasted_iota(jnp.int32, (ROWS, W), 0)
    lane = lax.broadcasted_iota(jnp.int32, (ROWS, W), 1)
    frame, row = sub >> 4, sub & 15

    def taps(frame_in, row_in):
        a, b = frame_in - frame, row_in - row + 1
        valid = (a >= 0) & (a <= 2) & (b >= 0) & (b <= 2)
        return jnp.where(valid, 3 * a + b, -99)

    keeps = (
        jnp.where(frame == 0, keep_ref[0], 1.0),
        jnp.where(frame == 1, keep_ref[1], 1.0),
    )
    tap = taps((lane & 63) >> 4, lane & 15)
    for o in range(HID):
        rows = slice(o * ROWS, (o + 1) * ROWS)
        for e in range(3):
            value = jnp.zeros((ROWS, W), F32)
            for q in range(9):
                value = jnp.where(tap == q, one_in[o * 27 + q * 3 + e], value)
            for p in range(2):
                first, second = two_parts(value * keeps[p])
                one_ref[e, p, rows, 0:W] = first
                one_ref[e, p, rows, W : 2 * W] = second
        for p in range(2):
            bias_ref[p * W + o * ROWS : p * W + (o + 1) * ROWS, :] = bias_in[o] * keeps[p]
    for p in range(2):
        tap = taps(2 * p + ((lane >> 4) & 1), lane & 15) + 9 * (lane >> 5)
        code = jnp.where(taps(2 * p + ((lane >> 4) & 1), lane & 15) < 0, -1, tap)
        for e in range(3):
            value = jnp.zeros((ROWS, W), F32)
            for q in range(9 * HID):
                value = jnp.where(code == q, two_in[q * 3 + e], value)
            first, second = two_parts(value)
            for copy in range(2):
                cols = slice(copy * 2 * W + p * W, copy * 2 * W + (p + 1) * W)
                two_ref[e * ROWS : (e + 1) * ROWS, cols] = first
                two_ref[(3 + e) * ROWS : (4 + e) * ROWS, cols] = second


def prepare(keep, conv_one, conv_bias, conv_two):
    return pl.pallas_call(
        prepare_kernel,
        out_shape=(
            jax.ShapeDtypeStruct((3, 2, W, 2 * W), BF16),
            jax.ShapeDtypeStruct((2 * W, W), F32),
            jax.ShapeDtypeStruct((6 * ROWS, 4 * W), BF16),
        ),
        in_specs=[SMEM] * 4,
        out_specs=(VMEM,) * 3,
        compiler_params=pltpu.CompilerParams(vmem_limit_bytes=4 << 20),
        cost_estimate=pl.CostEstimate(flops=1 << 20, bytes_accessed=1 << 19, transcendentals=0),
        name="prepare",
    )(keep, conv_one.reshape(-1), conv_bias, conv_two.reshape(-1))


def from_left(x):
    lane = lax.broadcasted_iota(jnp.int32, (1, W), 1)
    return jnp.where(lane == 0, 0.0, pltpu.roll(x, 1, 1))


def from_right(x):
    lane = lax.broadcasted_iota(jnp.int32, (1, W), 1)
    return jnp.where(lane == W - 1, 0.0, pltpu.roll(x, W - 1, 1))


def convolve(before_ref, cost_ref, after_ref, one_ref, bias_ref, two_ref, spread, middle, write):
    steps = HALF // LEVELS

    def split(s):
        target = spread[s % 2]
        for k in range(LEVELS):
            j = s * LEVELS + k
            x = jnp.concatenate([before_ref[j], cost_ref[j], after_ref[j]], axis=0)
            for e, value in enumerate((from_left(x), x, from_right(x))):
                for q, part in enumerate(two_parts(value)):
                    target[e, q, :, k * W : (k + 1) * W] = part

    def first(s):
        source, target = spread[s % 2], middle[s % 2]
        for pair in range(2):
            rows = slice(32 * pair, 32 * pair + 64)
            total = None
            for e in range(3):
                parts = [source[e, q, rows, :] for q in range(2)]
                term = jnp.dot(one_ref[e, pair], jnp.concatenate(parts * 2, axis=0),
                               preferred_element_type=F32)
                total = term if total is None else total + term
            bias = bias_ref[W * pair : W * pair + W, :]
            hidden = jnp.maximum(total + jnp.concatenate([bias] * LEVELS, axis=1), 0.0)
            for q, part in enumerate(two_parts(hidden)):
                target[q * 2 * W + pair * W : q * 2 * W + (pair + 1) * W, :] = part

    def second(s):
        both = jnp.dot(two_ref[...], middle[s % 2][...], preferred_element_type=F32)
        both = both[: 3 * ROWS] + both[3 * ROWS :]
        for k in range(LEVELS):
            mine = both[:, k * W : (k + 1) * W]
            j = s * LEVELS + k
            write(j, cost_ref[j] + (
                from_left(mine[0:ROWS]) + mine[ROWS : 2 * ROWS] + from_right(mine[2 * ROWS :])))

    split(0)
    for s in range(steps + 1):
        if s + 1 < steps:
            split(s + 1)
        if s < steps:
            first(s)
        if s > 0:
            second(s - 1)


def high_kernel(before_ref, cost_ref, after_ref, one_ref, bias_ref, two_ref, agg_ref,
                spread_0, spread_1, middle_0, middle_1):
    def write(j, value):
        agg_ref[j] = value

    convolve(before_ref, cost_ref, after_ref, one_ref, bias_ref, two_ref,
             (spread_0, spread_1), (middle_0, middle_1), write)


def low_kernel(base_ref, before_ref, cost_ref, after_ref, one_ref, bias_ref, two_ref, high_ref,
               out_ref, spread_0, spread_1, middle_0, middle_1, agg_s):
    def write(j, value):
        agg_s[j] = value

    convolve(before_ref, cost_ref, after_ref, one_ref, bias_ref, two_ref,
             (spread_0, spread_1), (middle_0, middle_1), write)

    base = base_ref[0].astype(F32)

    def aggregated(j):
        return agg_s[j] if j < HALF else high_ref[j - HALF]

    largest = aggregated(0)
    for j in range(1, NDISP):
        largest = jnp.maximum(largest, aggregated(j))
    weight = jnp.zeros((ROWS, W), F32)
    moment = jnp.zeros((ROWS, W), F32)
    for j in range(NDISP):
        e = jnp.exp(aggregated(j) - largest)
        weight = weight + e
        moment = moment + e * (base + float(j))
    out_ref[...] = moment / weight


CONV_SCRATCH = [
    pltpu.VMEM((3, 2, 3 * ROWS, LEVELS * W), BF16),
    pltpu.VMEM((3, 2, 3 * ROWS, LEVELS * W), BF16),
    pltpu.VMEM((4 * W, LEVELS * W), BF16),
    pltpu.VMEM((4 * W, LEVELS * W), BF16),
]


def aggregate_high(before, cost, after, one, bias, two):
    return pl.pallas_call(
        high_kernel,
        out_shape=jax.ShapeDtypeStruct((HALF, ROWS, W), F32),
        in_specs=[VMEM] * 6,
        out_specs=VMEM,
        scratch_shapes=CONV_SCRATCH,
        compiler_params=pltpu.CompilerParams(vmem_limit_bytes=12 << 20),
        cost_estimate=pl.CostEstimate(flops=2 << 30, bytes_accessed=2 << 20, transcendentals=0),
        name="aggregate_high",
    )(before, cost, after, one, bias, two)


def aggregate_low(base, before, cost, after, one, bias, two, high):
    return pl.pallas_call(
        low_kernel,
        out_shape=jax.ShapeDtypeStruct((ROWS, W), F32),
        in_specs=[SMEM] + [VMEM] * 7,
        out_specs=VMEM,
        scratch_shapes=CONV_SCRATCH + [pltpu.VMEM((HALF, ROWS, W), F32)],
        compiler_params=pltpu.CompilerParams(vmem_limit_bytes=12 << 20),
        cost_estimate=pl.CostEstimate(flops=2 << 30, bytes_accessed=2 << 20, transcendentals=0),
        name="aggregate_low",
    )(base, before, cost, after, one, bias, two, high)


def shards(features, disparity_base, conv_one, conv_bias, conv_two):
    own = features[0]
    cameras = lax.axis_size("cam")
    row_step = cameras // RIG_COLS
    right = passed_along(own, "cam", -1)
    left = passed_along(own, "cam", 1)
    down = passed_along(own, "cam", -row_step)
    up = passed_along(own, "cam", row_step)
    cost_high, low = across(disparity_base, own, right, left)
    before_high = shifted_along(cost_high, "tm", 1)
    after_high = shifted_along(cost_high, "tm", -1)
    cost_low = along(disparity_base, low, own, down, up)
    before_low = shifted_along(cost_low, "tm", 1)
    after_low = shifted_along(cost_low, "tm", -1)
    conv_one, conv_bias, conv_two, _ = lax.optimization_barrier(
        (conv_one, conv_bias, conv_two, cost_low))
    place = lax.axis_index("tm")
    keep = jnp.stack([place > 0, place < lax.axis_size("tm") - 1]).astype(F32)
    one, bias, two = prepare(keep, conv_one, conv_bias, conv_two)
    high = aggregate_high(before_high, cost_high, after_high, one, bias, two)
    out = aggregate_low(disparity_base, before_low, cost_low, after_low, one, bias, two, high)
    return out.reshape(1, T, H, W)


def solution(mesh):
    in_specs = (P("cam", None, "tm", None, None), P(), P(), P(), P())
    out_specs = P("cam", "tm", None, None)
    return jax.shard_map(shards, mesh=mesh, in_specs=in_specs, out_specs=out_specs, check_vma=False)
```

```python
import functools
import math

import jax
import jax.numpy as jnp
from jax import lax
from jax.experimental import pallas as pl
from jax.experimental.pallas import tpu as pltpu
from jax.sharding import PartitionSpec as P


NDISP = 32
HALF = NDISP // 2
RIG_COLS = 4
HID = 4
C = 32
T = 2
H = 16
W = 128
ROWS = T * H
PITCH = ROWS + 1
GROUP = 4
LEVELS = 2
FACTOR = 1.0 / math.sqrt(C) / 4.0
F32 = jnp.float32
BF16 = jnp.bfloat16
VMEM = pl.BlockSpec(memory_space=pltpu.VMEM)
SMEM = pl.BlockSpec(memory_space=pltpu.SMEM)
ANY = pl.BlockSpec(memory_space=pl.ANY)


def swapped(block, partner):
    return lax.ppermute(block, "cam", [(partner(k), k) for k in range(lax.axis_size("cam"))])


def shifted_along(block, axis, distance):
    count = lax.axis_size(axis)
    route = [(i, i + distance) for i in range(count) if 0 <= i + distance < count]
    return lax.ppermute(block, axis, route)


def two_parts(x):
    first = x.astype(BF16)
    return first, (x - first.astype(F32)).astype(BF16)


def widened(source, target):
    def step(i, carry):
        for k in range(4):
            c = i * 4 + k
            target[pl.ds(c * PITCH, ROWS), :] = source[c].reshape(ROWS, W).astype(F32)
        return carry

    lax.fori_loop(0, C // 4, step, 0)


def turned_group(source, g):
    return [
        source[pl.ds(g * GROUP + i, C, stride=PITCH), :].astype(BF16) for i in range(GROUP)
    ]


def correlate(base, mirrored, turned_ref, partner_s, grams, horiz_s):
    row = lax.broadcasted_iota(jnp.int32, (W, W), 0)
    col = lax.broadcasted_iota(jnp.int32, (W, W), 1)
    turn = (row == jnp.where(mirrored == 1, W - 1 - col, col)).astype(BF16)
    lane = lax.broadcasted_iota(jnp.int32, (8, W), 1)
    sub = lax.broadcasted_iota(jnp.int32, (8, W), 0)
    offset = jnp.where(mirrored == 1, W - 1 - lane, lane) + base
    index = (sub + offset) & 7
    stay = sub + (offset & 7) < 8
    inside = offset < W

    def products(g):
        partner = lax.dot_general(
            turn, jnp.concatenate(turned_group(partner_s, g), axis=0), (((1,), (1,)), ((), ())),
            preferred_element_type=F32).astype(BF16)
        mine = [turned_ref[g * W + i * C : g * W + (i + 1) * C, :] for i in range(GROUP)]
        blank = jnp.zeros((C, W), BF16)
        blocks = jnp.concatenate(
            [
                jnp.concatenate([mine[i] if i == k else blank for k in range(GROUP)], axis=1)
                for i in range(GROUP)
            ],
            axis=0,
        )
        grams[g % 2][...] = jnp.dot(partner, blocks, preferred_element_type=F32)

    def shift(g):
        gram = grams[g % 2]
        for i in range(GROUP):
            tiles = [gram[8 * k : 8 * k + 8, i * W : (i + 1) * W] for k in range(W // 8)]
            tiles += [jnp.zeros((8, W), F32)] * 4
            for bit, count in ((6, 12), (5, 8), (4, 6), (3, 5)):
                step = 1 << (bit - 3)
                take = (offset & (1 << bit)) != 0
                tiles = [jnp.where(take, tiles[k + step], tiles[k]) for k in range(count)]
            tiles = [
                jnp.take_along_axis(tile, index, axis=0, mode="promise_in_bounds") for tile in tiles
            ]
            for k in range(NDISP // 8):
                value = jnp.where(inside, jnp.where(stay, tiles[k], tiles[k + 1]), 0.0)
                horiz_s[pl.ds((g * GROUP + i) * PITCH + 8 * k, 8), :] = value

    groups = ROWS // GROUP
    products(0)
    for g in range(groups):
        if g + 1 < groups:
            products(g + 1)
        shift(g)


def near_kernel(base_ref, own_hbm, near_ref, turned_ref, part_ref,
                own_ref, sem, own_s, near_s, gram_0, gram_1, horiz_s):
    fetch = pltpu.make_async_copy(own_hbm, own_ref, sem)
    fetch.start()
    widened(near_ref, near_s)
    fetch.wait()
    widened(own_ref, own_s)
    for g in range(ROWS // GROUP):
        turned_ref[g * W : (g + 1) * W, :] = jnp.concatenate(turned_group(own_s, g), axis=0)
    correlate(base_ref[0], 1 - lax.axis_index("cam") % 2, turned_ref, near_s,
              (gram_0, gram_1), horiz_s)
    for level in range(NDISP):
        part_ref[level] = horiz_s[pl.ds(level, ROWS, stride=PITCH), :]


def next_kernel(base_ref, turned_ref, next_ref, part_ref, high_ref, low_ref,
                next_s, gram_0, gram_1, horiz_s):
    widened(next_ref, next_s)
    correlate(base_ref[0], lax.axis_index("cam") % 2, turned_ref, next_s,
              (gram_0, gram_1), horiz_s)
    for level in range(NDISP):
        summed = (part_ref[level] + horiz_s[pl.ds(level, ROWS, stride=PITCH), :]) * FACTOR
        if level < HALF:
            low_ref[level] = summed
        else:
            high_ref[level - HALF] = summed


FLAT = pltpu.VMEM((C * PITCH, W), F32)
GRAM = pltpu.VMEM((W, GROUP * W), F32)


def with_near(base, own, near):
    return pl.pallas_call(
        near_kernel,
        out_shape=(jax.ShapeDtypeStruct((ROWS * C, W), BF16),
                   jax.ShapeDtypeStruct((NDISP, ROWS, W), F32)),
        in_specs=[SMEM, ANY, VMEM],
        out_specs=(VMEM, VMEM),
        scratch_shapes=[pltpu.VMEM((C, T, H, W), BF16), pltpu.SemaphoreType.DMA,
                        FLAT, FLAT, GRAM, GRAM, FLAT],
        compiler_params=pltpu.CompilerParams(vmem_limit_bytes=12 << 20),
        cost_estimate=pl.CostEstimate(flops=1 << 30, bytes_accessed=2 << 20, transcendentals=0),
        name="with_near",
    )(base, own, near)


def with_next(base, turned, following, part):
    half = jax.ShapeDtypeStruct((HALF, ROWS, W), F32)
    return pl.pallas_call(
        next_kernel,
        out_shape=(half, half),
        in_specs=[SMEM, VMEM, VMEM, VMEM],
        out_specs=(VMEM, VMEM),
        scratch_shapes=[FLAT, GRAM, GRAM, FLAT],
        compiler_params=pltpu.CompilerParams(vmem_limit_bytes=12 << 20),
        cost_estimate=pl.CostEstimate(flops=1 << 30, bytes_accessed=2 << 20, transcendentals=0),
        name="with_next",
    )(base, turned, following, part)


def along_kernel(row_step, base_ref, own_ref, low_ref, same_ref, other_ref, cost_ref,
                 pair_s, vert_s):
    base = base_ref[0]
    half = H // 2
    size = C * T * 2 * H + H
    same_at = ((lax.axis_index("cam") // row_step) % 2) * size
    other_at = size - same_at
    zeros = jnp.zeros((H, W), F32)
    for start in (0, size):
        pair_s[start : start + H, :] = zeros

    def widen(i, carry):
        for k in range(2):
            c = i * 2 + k
            for source, at in ((same_ref, same_at), (other_ref, other_at)):
                for t in range(T):
                    start = pl.multiple_of(at + (c * T + t) * 2 * H + H, H)
                    pair_s[pl.ds(start, H), :] = source[c, t].astype(F32)
                    pair_s[pl.ds(start + H, H), :] = zeros
        return carry

    lax.fori_loop(0, C // 2, widen, 0)

    for t in range(T):

        def channels(i, sums, t=t):
            for k in range(4):
                c = i * 4 + k
                mine = own_ref[c, t].astype(F32)
                mine_low, mine_high = mine[:half], mine[half:]
                start = (c * T + t) * 2 * H + H
                results = []
                for level in range(H):
                    low, high = sums[2 * level], sums[2 * level + 1]
                    part_low = pair_s[pl.ds(size + start + level, half), :]
                    part_high = pair_s[pl.ds(start + half - level, half), :]
                    if level < half:
                        part_low = part_low + pair_s[pl.ds(start - level, half), :]
                        part_high = part_high + pair_s[pl.ds(size + start + half + level, half), :]
                    results += [low + mine_low * part_low, high + mine_high * part_high]
                sums = tuple(results)
            return sums

        sums = lax.fori_loop(0, C // 4, channels,
                             tuple(jnp.zeros((half, W), F32) for _ in range(2 * H)))
        for level in range(H):
            vert_s[level, t * H : t * H + half, :] = sums[2 * level]
            vert_s[level, t * H + half : (t + 1) * H, :] = sums[2 * level + 1]
    for level in range(H, H + 4):
        vert_s[level] = jnp.zeros((ROWS, W), F32)
    for level in range(HALF):
        cost_ref[level] = low_ref[level] + vert_s[base + level] * FACTOR


def along(row_step, base, own, low, same, other):
    padded = pltpu.VMEM((2 * (C * T * 2 * H + H), W), F32)
    return pl.pallas_call(
        functools.partial(along_kernel, row_step),
        out_shape=jax.ShapeDtypeStruct((HALF, ROWS, W), F32),
        in_specs=[SMEM] + [VMEM] * 4,
        out_specs=VMEM,
        scratch_shapes=[padded, pltpu.VMEM((H + 4, ROWS, W), F32)],
        compiler_params=pltpu.CompilerParams(vmem_limit_bytes=12 << 20),
        cost_estimate=pl.CostEstimate(flops=2 << 30, bytes_accessed=2 << 20, transcendentals=0),
        name="along",
    )(base, own, low, same, other)


def prepare_kernel(last, one_hbm, bias_hbm, two_hbm, one_ref, bias_ref, two_ref,
                   one_in, bias_in, two_in, sems):
    fetches = [
        pltpu.make_async_copy(source, target, sems.at[k])
        for k, (source, target) in enumerate(
            ((one_hbm, one_in), (bias_hbm, bias_in), (two_hbm, two_in)))
    ]
    for fetch in fetches:
        fetch.start()
    for fetch in fetches:
        fetch.wait()
    place = lax.axis_index("tm")
    keep_first = jnp.where(place > 0, 1.0, 0.0)
    keep_last = jnp.where(place < last, 1.0, 0.0)
    sub = lax.broadcasted_iota(jnp.int32, (ROWS, W), 0)
    lane = lax.broadcasted_iota(jnp.int32, (ROWS, W), 1)
    frame, row = sub >> 4, sub & 15

    def taps(frame_in, row_in):
        a, b = frame_in - frame, row_in - row + 1
        valid = (a >= 0) & (a <= 2) & (b >= 0) & (b <= 2)
        return jnp.where(valid, 3 * a + b, -99)

    keeps = (
        jnp.where(frame == 0, keep_first, 1.0),
        jnp.where(frame == 1, keep_last, 1.0),
    )
    tap = taps((lane & 63) >> 4, lane & 15)
    for o in range(HID):
        rows = slice(o * ROWS, (o + 1) * ROWS)
        for e in range(3):
            value = jnp.zeros((ROWS, W), F32)
            for q in range(9):
                value = jnp.where(tap == q, one_in[q // 3, q % 3, o, e], value)
            for p in range(2):
                first, second = two_parts(value * keeps[p])
                one_ref[e, p, rows, 0:W] = first
                one_ref[e, p, rows, W : 2 * W] = second
        for p in range(2):
            bias_ref[p * W + o * ROWS : p * W + (o + 1) * ROWS, :] = bias_in[o] * keeps[p]
    for p in range(2):
        tap = taps(2 * p + ((lane >> 4) & 1), lane & 15) + 9 * (lane >> 5)
        code = jnp.where(taps(2 * p + ((lane >> 4) & 1), lane & 15) < 0, -1, tap)
        for e in range(3):
            value = jnp.zeros((ROWS, W), F32)
            for q in range(9 * HID):
                value = jnp.where(code == q, two_in[(q % 9) // 3, q % 3, q // 9, e], value)
            first, second = two_parts(value)
            for copy in range(2):
                cols = slice(copy * W, (copy + 1) * W)
                two_ref[p, e * ROWS : (e + 1) * ROWS, cols] = first
                two_ref[p, (3 + e) * ROWS : (4 + e) * ROWS, cols] = second


def prepare(last, conv_one, conv_bias, conv_two):
    return pl.pallas_call(
        functools.partial(prepare_kernel, last),
        out_shape=(
            jax.ShapeDtypeStruct((3, 2, W, 2 * W), BF16),
            jax.ShapeDtypeStruct((2 * W, W), F32),
            jax.ShapeDtypeStruct((2, 6 * ROWS, 2 * W), BF16),
        ),
        in_specs=[ANY] * 3,
        out_specs=(VMEM,) * 3,
        scratch_shapes=[pltpu.SMEM((3, 3, HID, 3), F32), pltpu.SMEM((HID,), F32),
                        pltpu.SMEM((3, 3, HID, 3), F32), pltpu.SemaphoreType.DMA((3,))],
        compiler_params=pltpu.CompilerParams(vmem_limit_bytes=6 << 20),
        cost_estimate=pl.CostEstimate(flops=1 << 20, bytes_accessed=1 << 19, transcendentals=0),
        name="prepare",
    )(*(pltpu.with_memory_space_constraint(x, pltpu.HBM) for x in (
        conv_one.transpose(1, 2, 0, 3), conv_bias, conv_two.transpose(1, 2, 0, 3))))


def from_left(x):
    lane = lax.broadcasted_iota(jnp.int32, (1, W), 1)
    return jnp.where(lane == 0, 0.0, pltpu.roll(x, 1, 1))


def from_right(x):
    lane = lax.broadcasted_iota(jnp.int32, (1, W), 1)
    return jnp.where(lane == W - 1, 0.0, pltpu.roll(x, W - 1, 1))


def convolve(pairs, frames, one_ref, bias_ref, two_ref, scratch, write):
    steps = HALF // LEVELS
    spread, middle = scratch[:2], scratch[2:]

    def split(s):
        target = spread[s % 2]
        for k in range(LEVELS):
            x = jnp.concatenate([ref[s * LEVELS + k] for ref in frames], axis=0)
            for e, value in enumerate((from_left(x), x, from_right(x))):
                for q, part in enumerate(two_parts(value)):
                    target[e, q, 0 : len(frames) * ROWS, k * W : (k + 1) * W] = part

    def first(s):
        source, target = spread[s % 2], middle[s % 2]
        for place, pair in enumerate(pairs):
            rows = slice(ROWS * place, ROWS * place + 2 * ROWS)
            total = None
            for e in range(3):
                parts = [source[e, q, rows, :] for q in range(2)]
                term = jnp.dot(one_ref[e, pair], jnp.concatenate(parts * 2, axis=0),
                               preferred_element_type=F32)
                total = term if total is None else total + term
            bias = bias_ref[W * pair : W * pair + W, :]
            hidden = jnp.maximum(total + jnp.concatenate([bias] * LEVELS, axis=1), 0.0)
            for q, part in enumerate(two_parts(hidden)):
                target[place, q * W : (q + 1) * W, :] = part

    def second(s):
        total = None
        for place, pair in enumerate(pairs):
            term = jnp.dot(two_ref[pair], middle[s % 2][place], preferred_element_type=F32)
            total = term if total is None else total + term
        both = total[: 3 * ROWS] + total[3 * ROWS :]
        for k in range(LEVELS):
            mine = both[:, k * W : (k + 1) * W]
            write(s * LEVELS + k, (
                from_left(mine[0:ROWS]) + mine[ROWS : 2 * ROWS] + from_right(mine[2 * ROWS :])))

    split(0)
    for s in range(steps + 1):
        if s + 1 < steps:
            split(s + 1)
        if s < steps:
            first(s)
        if s > 0:
            second(s - 1)


def softened(agg_ref, lowest):
    largest = agg_ref[0]
    for j in range(1, HALF):
        largest = jnp.maximum(largest, agg_ref[j])
    weight = jnp.zeros((ROWS, W), F32)
    moment = jnp.zeros((ROWS, W), F32)
    for j in range(HALF):
        e = jnp.exp(agg_ref[j] - largest)
        weight = weight + e
        moment = moment + e * (lowest + float(j))
    return largest, weight, moment


def high_kernel(base_ref, before_ref, cost_ref, after_ref, one_ref, bias_ref, two_ref, out_ref,
                agg_s, *scratch):
    def write(j, value):
        agg_s[j] = cost_ref[j] + value

    convolve((0, 1), (before_ref, cost_ref, after_ref), one_ref, bias_ref, two_ref, scratch, write)
    lowest = base_ref[0].astype(F32) + float(HALF)
    for k, value in enumerate(softened(agg_s, lowest)):
        out_ref[k] = value


def early_kernel(before_ref, cost_ref, one_ref, bias_ref, two_ref, agg_ref, *scratch):
    def write(j, value):
        agg_ref[j] = cost_ref[j] + value

    convolve((0,), (before_ref, cost_ref), one_ref, bias_ref, two_ref, scratch, write)


def late_kernel(base_ref, cost_ref, after_ref, one_ref, bias_ref, two_ref, early_ref, high_ref,
                out_ref, agg_s, *scratch):
    def write(j, value):
        agg_s[j] = early_ref[j] + value

    convolve((1,), (cost_ref, after_ref), one_ref, bias_ref, two_ref, scratch, write)
    largest, weight, moment = softened(agg_s, base_ref[0].astype(F32))
    top = jnp.maximum(largest, high_ref[0])
    low_part, high_part = jnp.exp(largest - top), jnp.exp(high_ref[0] - top)
    weight = weight * low_part + high_ref[1] * high_part
    out_ref[...] = (moment * low_part + high_ref[2] * high_part) / weight


def conv_call(kernel, out_shape, in_specs, pairs, own_sums, *operands):
    spread = pltpu.VMEM((3, 2, (pairs + 1) * ROWS, LEVELS * W), BF16)
    middle = pltpu.VMEM((pairs, 2 * W, LEVELS * W), BF16)
    sums = [pltpu.VMEM((HALF, ROWS, W), F32)] if own_sums else []
    return pl.pallas_call(
        kernel,
        out_shape=jax.ShapeDtypeStruct(out_shape, F32),
        in_specs=in_specs,
        out_specs=VMEM,
        scratch_shapes=sums + [spread, spread, middle, middle],
        compiler_params=pltpu.CompilerParams(vmem_limit_bytes=12 << 20),
        cost_estimate=pl.CostEstimate(
            flops=pairs << 30, bytes_accessed=1 << 20, transcendentals=0),
    )(*operands)


def shards(features, disparity_base, conv_one, conv_bias, conv_two):
    own = features[0]
    cameras = lax.axis_size("cam")
    row_step = cameras // RIG_COLS
    same = swapped(own, lambda k: k ^ row_step)
    near = swapped(own, lambda k: k ^ 1)
    following = swapped(own, lambda k: (k - 1 + 2 * (k % 2)) % cameras)
    other = swapped(same, lambda k: k ^ (2 * row_step))
    turned, part = with_near(
        disparity_base, pltpu.with_memory_space_constraint(own, pltpu.HBM), near)
    cost_high, low = with_next(disparity_base, turned, following, part)
    before_high = shifted_along(cost_high, "tm", 1)
    after_high = shifted_along(cost_high, "tm", -1)
    cost_low = along(row_step, disparity_base, own, low, same, other)
    before_low = shifted_along(cost_low, "tm", 1)
    after_low = shifted_along(cost_low, "tm", -1)
    matrices = prepare(lax.axis_size("tm") - 1, conv_one, conv_bias, conv_two)
    high = conv_call(high_kernel, (3, ROWS, W), [SMEM] + [VMEM] * 6, 2, True,
                     disparity_base, before_high, cost_high, after_high, *matrices)
    early = conv_call(early_kernel, (HALF, ROWS, W), [VMEM] * 5, 1, False,
                      before_low, cost_low, *matrices)
    out = conv_call(late_kernel, (ROWS, W), [SMEM] + [VMEM] * 7, 1, True,
                    disparity_base, cost_low, after_low, *matrices, early, high)
    return out.reshape(1, T, H, W)


def solution(mesh):
    in_specs = (P("cam", None, "tm", None, None), P(), P(), P(), P())
    out_specs = P("cam", "tm", None, None)
    return jax.shard_map(shards, mesh=mesh, in_specs=in_specs, out_specs=out_specs, check_vma=False)
```

```python
import functools
import math

import jax
import jax.numpy as jnp
from jax import lax
from jax.experimental import pallas as pl
from jax.experimental.pallas import tpu as pltpu
from jax.sharding import PartitionSpec as P


NDISP = 32
HALF = NDISP // 2
RIG_COLS = 4
HID = 4
C = 32
T = 2
H = 16
W = 128
ROWS = T * H
HALF_WORDS = HALF // 4 * 3 * ROWS
PITCH = ROWS + 1
GROUP = 4
LEVELS = 8
FACTOR = 1.0 / math.sqrt(C) / 4.0
F32 = jnp.float32
BF16 = jnp.bfloat16
VMEM = pl.BlockSpec(memory_space=pltpu.VMEM)
SMEM = pl.BlockSpec(memory_space=pltpu.SMEM)
ANY = pl.BlockSpec(memory_space=pl.ANY)


def swapped(block, partner):
    return lax.ppermute(block, "cam", [(partner(k), k) for k in range(lax.axis_size("cam"))])


def shifted_along(block, axis, distance):
    count = lax.axis_size(axis)
    route = [(i, i + distance) for i in range(count) if 0 <= i + distance < count]
    return lax.ppermute(block, axis, route)


def two_parts(x):
    first = x.astype(BF16)
    return first, (x - first.astype(F32)).astype(BF16)


LOWEST_POWER, HIGHEST_POWER = -24, 15


def largest_of(planes):
    top = jnp.abs(planes[0])
    for plane in planes[1:]:
        top = jnp.maximum(top, jnp.abs(plane))
    return jnp.broadcast_to(jnp.max(top, axis=(0, 1), keepdims=True), (8, W))


def power_of(top):
    power = jnp.full((8, W), LOWEST_POWER - 1, jnp.int32)
    for k in range(LOWEST_POWER, HIGHEST_POWER + 1):
        power = jnp.where(top >= 2.0**k, k, power)
    return power


def by_power(power, sign, bits):
    factor = jnp.full((8, W), 2.0 ** (sign * (bits - LOWEST_POWER + 1)), F32)
    for k in range(LOWEST_POWER, HIGHEST_POWER + 1):
        factor = jnp.where(power >= k, 2.0 ** (sign * (bits - k)), factor)
    return jnp.concatenate([factor] * (ROWS // 8), axis=0)


def packed(planes, power):
    factor = by_power(power, 1, 22)
    words = []
    for i in range(0, len(planes), 4):
        q = [
            jnp.minimum(jnp.floor(plane * factor + 0.5), 2.0**23 - 1).astype(jnp.int32)
            for plane in planes[i : i + 4]
        ]
        last = (q[3] & 255, (q[3] >> 8) & 255, (q[3] >> 16) & 255)
        words += [(q[k] << 8) | last[k] for k in range(3)]
    return words


def unpack(source, start, power_at, target, place, levels):
    factor = by_power(source[power_at : power_at + 8, :], -1, 22)
    for i in range(0, levels, 4):
        at = start + i // 4 * 3 * ROWS
        words = [source[at + k * ROWS : at + (k + 1) * ROWS, :] for k in range(3)]
        last = ((words[2] & 255) << 24) | ((words[1] & 255) << 16) | ((words[0] & 255) << 8)
        for k, q in enumerate([word >> 8 for word in words] + [last >> 8]):
            target[place + i + k] = q.astype(F32) * factor


def put(target, start, words):
    for k, word in enumerate(words):
        target[start + k * ROWS : start + (k + 1) * ROWS, :] = word


def coded(levels, powers=1):
    return jax.ShapeDtypeStruct((levels // 4 * 3 * ROWS + 8 * powers, W), jnp.int32)


def widened(source, target):
    def step(i, carry):
        for k in range(4):
            c = i * 4 + k
            target[pl.ds(c * PITCH, ROWS), :] = source[c].reshape(ROWS, W).astype(F32)
        return carry

    lax.fori_loop(0, C // 4, step, 0)


def turned_group(source, g):
    return [
        source[pl.ds(g * GROUP + i, C, stride=PITCH), :].astype(BF16) for i in range(GROUP)
    ]


def correlate(base, mirrored, turned_ref, partner_s, grams, horiz_s):
    row = lax.broadcasted_iota(jnp.int32, (W, W), 0)
    col = lax.broadcasted_iota(jnp.int32, (W, W), 1)
    turn = (row == jnp.where(mirrored == 1, W - 1 - col, col)).astype(BF16)
    lane = lax.broadcasted_iota(jnp.int32, (8, W), 1)
    sub = lax.broadcasted_iota(jnp.int32, (8, W), 0)
    offset = jnp.where(mirrored == 1, W - 1 - lane, lane) + base
    index = (sub + offset) & 7
    stay = sub + (offset & 7) < 8
    inside = offset < W

    def products(g):
        partner = lax.dot_general(
            turn, jnp.concatenate(turned_group(partner_s, g), axis=0), (((1,), (1,)), ((), ())),
            preferred_element_type=F32).astype(BF16)
        mine = [turned_ref[g * W + i * C : g * W + (i + 1) * C, :] for i in range(GROUP)]
        blank = jnp.zeros((C, W), BF16)
        blocks = jnp.concatenate(
            [
                jnp.concatenate([mine[i] if i == k else blank for k in range(GROUP)], axis=1)
                for i in range(GROUP)
            ],
            axis=0,
        )
        grams[g % 2][...] = jnp.dot(partner, blocks, preferred_element_type=F32)

    def shift(g):
        gram = grams[g % 2]
        for i in range(GROUP):
            tiles = [gram[8 * k : 8 * k + 8, i * W : (i + 1) * W] for k in range(W // 8)]
            tiles += [jnp.zeros((8, W), F32)] * 4
            for bit, count in ((6, 12), (5, 8), (4, 6), (3, 5)):
                step = 1 << (bit - 3)
                take = (offset & (1 << bit)) != 0
                tiles = [jnp.where(take, tiles[k + step], tiles[k]) for k in range(count)]
            tiles = [
                jnp.take_along_axis(tile, index, axis=0, mode="promise_in_bounds") for tile in tiles
            ]
            for k in range(NDISP // 8):
                value = jnp.where(inside, jnp.where(stay, tiles[k], tiles[k + 1]), 0.0)
                horiz_s[pl.ds((g * GROUP + i) * PITCH + 8 * k, 8), :] = value

    groups = ROWS // GROUP
    products(0)
    for g in range(groups):
        if g + 1 < groups:
            products(g + 1)
        shift(g)


def near_kernel(base_ref, own_hbm, near_ref, turned_ref, part_ref,
                own_ref, sem, own_s, near_s, gram_0, gram_1, horiz_s):
    fetch = pltpu.make_async_copy(own_hbm, own_ref, sem)
    fetch.start()
    widened(near_ref, near_s)
    fetch.wait()
    widened(own_ref, own_s)
    for g in range(ROWS // GROUP):
        turned_ref[g * W : (g + 1) * W, :] = jnp.concatenate(turned_group(own_s, g), axis=0)
    correlate(base_ref[0], 1 - lax.axis_index("cam") % 2, turned_ref, near_s,
              (gram_0, gram_1), horiz_s)
    for level in range(NDISP):
        part_ref[level] = horiz_s[pl.ds(level, ROWS, stride=PITCH), :]


def next_kernel(base_ref, turned_ref, next_ref, part_ref, high_ref, low_ref, code_ref,
                next_s, gram_0, gram_1, horiz_s):
    widened(next_ref, next_s)
    correlate(base_ref[0], lax.axis_index("cam") % 2, turned_ref, next_s,
              (gram_0, gram_1), horiz_s)
    for level in range(NDISP):
        summed = (part_ref[level] + horiz_s[pl.ds(level, ROWS, stride=PITCH), :]) * FACTOR
        if level < HALF:
            low_ref[level] = summed
        else:
            high_ref[level - HALF] = summed
    planes = [high_ref[k] for k in range(HALF)]
    power = power_of(largest_of(planes))
    put(code_ref, 0, packed(planes, power))
    code_ref[HALF_WORDS : HALF_WORDS + 8, :] = power


FLAT = pltpu.VMEM((C * PITCH, W), F32)
GRAM = pltpu.VMEM((W, GROUP * W), F32)


def with_near(base, own, near):
    return pl.pallas_call(
        near_kernel,
        out_shape=(jax.ShapeDtypeStruct((ROWS * C, W), BF16),
                   jax.ShapeDtypeStruct((NDISP, ROWS, W), F32)),
        in_specs=[SMEM, ANY, VMEM],
        out_specs=(VMEM, VMEM),
        scratch_shapes=[pltpu.VMEM((C, T, H, W), BF16), pltpu.SemaphoreType.DMA,
                        FLAT, FLAT, GRAM, GRAM, FLAT],
        compiler_params=pltpu.CompilerParams(vmem_limit_bytes=12 << 20),
        cost_estimate=pl.CostEstimate(flops=1 << 30, bytes_accessed=2 << 20, transcendentals=0),
        name="with_near",
    )(base, own, near)


def with_next(base, turned, following, part):
    half = jax.ShapeDtypeStruct((HALF, ROWS, W), F32)
    return pl.pallas_call(
        next_kernel,
        out_shape=(half, half, coded(HALF)),
        in_specs=[SMEM, VMEM, VMEM, VMEM],
        out_specs=(VMEM, VMEM, VMEM),
        scratch_shapes=[FLAT, GRAM, GRAM, FLAT],
        compiler_params=pltpu.CompilerParams(vmem_limit_bytes=12 << 20),
        cost_estimate=pl.CostEstimate(flops=1 << 30, bytes_accessed=2 << 20, transcendentals=0),
        name="with_next",
    )(base, turned, following, part)


def along_kernel(row_step, base_ref, own_ref, high_ref, low_ref, same_ref, other_ref,
                 cost_ref, code_ref, all_ref, pair_s, vert_s):
    base = base_ref[0]
    half = H // 2
    size = C * T * 2 * H + H
    same_at = ((lax.axis_index("cam") // row_step) % 2) * size
    other_at = size - same_at
    zeros = jnp.zeros((H, W), F32)
    for start in (0, size):
        pair_s[start : start + H, :] = zeros

    def widen(i, carry):
        for k in range(2):
            c = i * 2 + k
            for source, at in ((same_ref, same_at), (other_ref, other_at)):
                for t in range(T):
                    start = pl.multiple_of(at + (c * T + t) * 2 * H + H, H)
                    pair_s[pl.ds(start, H), :] = source[c, t].astype(F32)
                    pair_s[pl.ds(start + H, H), :] = zeros
        return carry

    lax.fori_loop(0, C // 2, widen, 0)

    for t in range(T):

        def channels(i, sums, t=t):
            for k in range(4):
                c = i * 4 + k
                mine = own_ref[c, t].astype(F32)
                mine_low, mine_high = mine[:half], mine[half:]
                start = (c * T + t) * 2 * H + H
                results = []
                for level in range(H):
                    low, high = sums[2 * level], sums[2 * level + 1]
                    part_low = pair_s[pl.ds(size + start + level, half), :]
                    part_high = pair_s[pl.ds(start + half - level, half), :]
                    if level < half:
                        part_low = part_low + pair_s[pl.ds(start - level, half), :]
                        part_high = part_high + pair_s[pl.ds(size + start + half + level, half), :]
                    results += [low + mine_low * part_low, high + mine_high * part_high]
                sums = tuple(results)
            return sums

        sums = lax.fori_loop(0, C // 4, channels,
                             tuple(jnp.zeros((half, W), F32) for _ in range(2 * H)))
        for level in range(H):
            vert_s[level, t * H : t * H + half, :] = sums[2 * level]
            vert_s[level, t * H + half : (t + 1) * H, :] = sums[2 * level + 1]
    for level in range(H, H + 4):
        vert_s[level] = jnp.zeros((ROWS, W), F32)
    for level in range(HALF):
        cost_ref[level] = low_ref[level] + vert_s[base + level] * FACTOR
    planes = [cost_ref[level] for level in range(HALF)]
    power = power_of(largest_of(planes))
    words = packed(planes, power)
    put(code_ref, 0, words)
    code_ref[HALF_WORDS : HALF_WORDS + 8, :] = power
    all_ref[0 : HALF_WORDS + 8, :] = high_ref[...]
    put(all_ref, HALF_WORDS + 8, words)
    all_ref[2 * HALF_WORDS + 8 :, :] = power


def along(row_step, base, own, high, low, same, other):
    padded = pltpu.VMEM((2 * (C * T * 2 * H + H), W), F32)
    return pl.pallas_call(
        functools.partial(along_kernel, row_step),
        out_shape=(jax.ShapeDtypeStruct((HALF, ROWS, W), F32), coded(HALF), coded(NDISP, 2)),
        in_specs=[SMEM] + [VMEM] * 5,
        out_specs=(VMEM,) * 3,
        scratch_shapes=[padded, pltpu.VMEM((H + 4, ROWS, W), F32)],
        compiler_params=pltpu.CompilerParams(vmem_limit_bytes=12 << 20),
        cost_estimate=pl.CostEstimate(flops=2 << 30, bytes_accessed=2 << 20, transcendentals=0),
        name="along",
    )(base, own, high, low, same, other)


def prepare_kernel(last, one_hbm, bias_hbm, two_hbm, one_ref, bias_ref, two_ref,
                   one_in, bias_in, two_in, sems):
    fetches = [
        pltpu.make_async_copy(source, target, sems.at[k])
        for k, (source, target) in enumerate(
            ((one_hbm, one_in), (bias_hbm, bias_in), (two_hbm, two_in)))
    ]
    for fetch in fetches:
        fetch.start()
    for fetch in fetches:
        fetch.wait()
    place = lax.axis_index("tm")
    keep_first = jnp.where(place > 0, 1.0, 0.0)
    keep_last = jnp.where(place < last, 1.0, 0.0)
    sub = lax.broadcasted_iota(jnp.int32, (ROWS, W), 0)
    lane = lax.broadcasted_iota(jnp.int32, (ROWS, W), 1)
    frame, row = sub >> 4, sub & 15

    def taps(frame_in, row_in):
        a, b = frame_in - frame, row_in - row + 1
        valid = (a >= 0) & (a <= 2) & (b >= 0) & (b <= 2)
        return jnp.where(valid, 3 * a + b, -99)

    keeps = (
        jnp.where(frame == 0, keep_first, 1.0),
        jnp.where(frame == 1, keep_last, 1.0),
    )
    tap = taps((lane & 63) >> 4, lane & 15)
    for o in range(HID):
        rows = slice(o * ROWS, (o + 1) * ROWS)
        for e in range(3):
            value = jnp.zeros((ROWS, W), F32)
            for q in range(9):
                value = jnp.where(tap == q, one_in[q // 3, q % 3, o, e], value)
            for p in range(2):
                first, second = two_parts(value * keeps[p])
                one_ref[e, p, rows, 0:W] = first
                one_ref[e, p, rows, W : 2 * W] = second
        for p in range(2):
            bias_ref[p * W + o * ROWS : p * W + (o + 1) * ROWS, :] = bias_in[o] * keeps[p]
    for p in range(2):
        tap = taps(2 * p + ((lane >> 4) & 1), lane & 15) + 9 * (lane >> 5)
        code = jnp.where(taps(2 * p + ((lane >> 4) & 1), lane & 15) < 0, -1, tap)
        for e in range(3):
            value = jnp.zeros((ROWS, W), F32)
            for q in range(9 * HID):
                value = jnp.where(code == q, two_in[(q % 9) // 3, q % 3, q // 9, e], value)
            first, second = two_parts(value)
            for copy in range(2):
                cols = slice(copy * W, (copy + 1) * W)
                two_ref[p, e * ROWS : (e + 1) * ROWS, cols] = first
                two_ref[p, (3 + e) * ROWS : (4 + e) * ROWS, cols] = second


def prepare(last, conv_one, conv_bias, conv_two):
    return pl.pallas_call(
        functools.partial(prepare_kernel, last),
        out_shape=(
            jax.ShapeDtypeStruct((3, 2, W, 2 * W), BF16),
            jax.ShapeDtypeStruct((2 * W, W), F32),
            jax.ShapeDtypeStruct((2, 6 * ROWS, 2 * W), BF16),
        ),
        in_specs=[ANY] * 3,
        out_specs=(VMEM,) * 3,
        scratch_shapes=[pltpu.SMEM((3, 3, HID, 3), F32), pltpu.SMEM((HID,), F32),
                        pltpu.SMEM((3, 3, HID, 3), F32), pltpu.SemaphoreType.DMA((3,))],
        compiler_params=pltpu.CompilerParams(vmem_limit_bytes=6 << 20),
        cost_estimate=pl.CostEstimate(flops=1 << 20, bytes_accessed=1 << 19, transcendentals=0),
        name="prepare",
    )(*(pltpu.with_memory_space_constraint(x, pltpu.HBM) for x in (
        conv_one.transpose(1, 2, 0, 3), conv_bias, conv_two.transpose(1, 2, 0, 3))))


def from_left(x):
    lane = lax.broadcasted_iota(jnp.int32, (1, W), 1)
    return jnp.where(lane == 0, 0.0, pltpu.roll(x, 1, 1))


def from_right(x):
    lane = lax.broadcasted_iota(jnp.int32, (1, W), 1)
    return jnp.where(lane == W - 1, 0.0, pltpu.roll(x, W - 1, 1))


def convolve(pair, frames, one_ref, bias_ref, two_ref, scratch, write):
    steps = NDISP // LEVELS
    spread, middle = scratch[:2], scratch[2:]

    def split(s):
        target = spread[s % 2]
        for k in range(LEVELS):
            x = jnp.concatenate([plane(s * LEVELS + k) for plane in frames], axis=0)
            for e, value in enumerate((from_left(x), x, from_right(x))):
                for q, part in enumerate(two_parts(value)):
                    target[e, q, :, k * W : (k + 1) * W] = part

    def first(s):
        source, target = spread[s % 2], middle[s % 2]
        total = None
        for e in range(3):
            parts = [source[e, q] for q in range(2)]
            term = jnp.dot(one_ref[e, pair], jnp.concatenate(parts * 2, axis=0),
                           preferred_element_type=F32)
            total = term if total is None else total + term
        bias = bias_ref[W * pair : W * pair + W, :]
        hidden = jnp.maximum(total + jnp.concatenate([bias] * LEVELS, axis=1), 0.0)
        for q, part in enumerate(two_parts(hidden)):
            target[q * W : (q + 1) * W, :] = part

    def second(s):
        total = jnp.dot(two_ref[pair], middle[s % 2][...], preferred_element_type=F32)
        both = total[: 3 * ROWS] + total[3 * ROWS :]
        for k in range(LEVELS):
            mine = both[:, k * W : (k + 1) * W]
            write(s * LEVELS + k, (
                from_left(mine[0:ROWS]) + mine[ROWS : 2 * ROWS] + from_right(mine[2 * ROWS :])))

    split(0)
    for s in range(steps + 1):
        if s + 1 < steps:
            split(s + 1)
        if s < steps:
            first(s)
        if s > 0:
            second(s - 1)


def early_kernel(low_code, high_code, low_ref, high_ref, one_ref, bias_ref, two_ref, agg_ref,
                 before_s, *scratch):
    unpack(low_code, 0, HALF_WORDS, before_s, 0, HALF)
    unpack(high_code, 0, HALF_WORDS, before_s, HALF, HALF)

    def cost(j):
        return low_ref[j] if j < HALF else high_ref[j - HALF]

    def write(j, value):
        agg_ref[j] = cost(j) + value

    convolve(0, (lambda j: before_s[j], cost), one_ref, bias_ref, two_ref, scratch, write)


def late_kernel(base_ref, code_ref, low_ref, high_ref, early_ref, one_ref, bias_ref, two_ref,
                out_ref, after_s, agg_s, *scratch):
    unpack(code_ref, HALF_WORDS + 8, 2 * HALF_WORDS + 8, after_s, 0, HALF)
    unpack(code_ref, 0, HALF_WORDS, after_s, HALF, HALF)

    def write(j, value):
        agg_s[j] = early_ref[j] + value

    def cost(j):
        return low_ref[j] if j < HALF else high_ref[j - HALF]

    convolve(1, (cost, lambda j: after_s[j]), one_ref, bias_ref, two_ref, scratch, write)

    base = base_ref[0].astype(F32)
    largest = agg_s[0]
    for j in range(1, NDISP):
        largest = jnp.maximum(largest, agg_s[j])
    weight = jnp.zeros((ROWS, W), F32)
    moment = jnp.zeros((ROWS, W), F32)
    for j in range(NDISP):
        e = jnp.exp(agg_s[j] - largest)
        weight = weight + e
        moment = moment + e * (base + float(j))
    out_ref[...] = moment / weight


def conv_call(kernel, out_shape, in_specs, sums, *operands):
    sums = [pltpu.VMEM((levels, ROWS, W), F32) for levels in sums]
    spread = pltpu.VMEM((3, 2, 2 * ROWS, LEVELS * W), BF16)
    middle = pltpu.VMEM((2 * W, LEVELS * W), BF16)
    return pl.pallas_call(
        kernel,
        out_shape=jax.ShapeDtypeStruct(out_shape, F32),
        in_specs=in_specs,
        out_specs=VMEM,
        scratch_shapes=sums + [spread, spread, middle, middle],
        compiler_params=pltpu.CompilerParams(vmem_limit_bytes=12 << 20),
        cost_estimate=pl.CostEstimate(
            flops=1 << 30, bytes_accessed=1 << 20, transcendentals=0),
    )(*operands)


def shards(features, disparity_base, conv_one, conv_bias, conv_two):
    own = features[0]
    cameras = lax.axis_size("cam")
    row_step = cameras // RIG_COLS
    same = swapped(own, lambda k: k ^ row_step)
    near = swapped(own, lambda k: k ^ 1)
    following = swapped(own, lambda k: (k - 1 + 2 * (k % 2)) % cameras)
    other = swapped(same, lambda k: k ^ (2 * row_step))
    turned, part = with_near(
        disparity_base, pltpu.with_memory_space_constraint(own, pltpu.HBM), near)
    cost_high, low, code_high = with_next(disparity_base, turned, following, part)
    before_high = shifted_along(code_high, "tm", 1)
    cost_low, code_low, code_all = along(
        row_step, disparity_base, own, code_high, low, same, other)
    before_low = shifted_along(code_low, "tm", 1)
    after = shifted_along(code_all, "tm", -1)
    matrices = prepare(lax.axis_size("tm") - 1, conv_one, conv_bias, conv_two)
    early = conv_call(early_kernel, (NDISP, ROWS, W), [VMEM] * 7, (NDISP,),
                      before_low, before_high, cost_low, cost_high,
                      *matrices)
    out = conv_call(late_kernel, (ROWS, W), [SMEM] + [VMEM] * 7, (NDISP, NDISP),
                    disparity_base, after, cost_low, cost_high, early,
                    *matrices)
    return out.reshape(1, T, H, W)


def solution(mesh):
    in_specs = (P("cam", None, "tm", None, None), P(), P(), P(), P())
    out_specs = P("cam", "tm", None, None)
    return jax.shard_map(shards, mesh=mesh, in_specs=in_specs, out_specs=out_specs, check_vma=False)
```

```python
import functools
import math

import jax
import jax.numpy as jnp
from jax import lax
from jax.experimental import pallas as pl
from jax.experimental.pallas import tpu as pltpu
from jax.sharding import PartitionSpec as P


NDISP = 32
HALF = NDISP // 2
RIG_COLS = 4
HID = 4
C = 32
T = 2
H = 16
W = 128
ROWS = T * H
HALF_WORDS = HALF // 4 * 3 * ROWS
PITCH = ROWS + 1
GROUP = 4
LEVELS = 8
FACTOR = 1.0 / math.sqrt(C) / 4.0
F32 = jnp.float32
BF16 = jnp.bfloat16
VMEM = pl.BlockSpec(memory_space=pltpu.VMEM)
SMEM = pl.BlockSpec(memory_space=pltpu.SMEM)
ANY = pl.BlockSpec(memory_space=pl.ANY)


def swapped(block, partner):
    return lax.ppermute(block, "cam", [(partner(k), k) for k in range(lax.axis_size("cam"))])


def shifted_along(block, axis, distance):
    count = lax.axis_size(axis)
    route = [(i, i + distance) for i in range(count) if 0 <= i + distance < count]
    return lax.ppermute(block, axis, route)


def two_parts(x):
    first = x.astype(BF16)
    return first, (x - first.astype(F32)).astype(BF16)


LOWEST_POWER, HIGHEST_POWER = -24, 15


def largest_of(planes):
    top = jnp.abs(planes[0])
    for plane in planes[1:]:
        top = jnp.maximum(top, jnp.abs(plane))
    return jnp.broadcast_to(jnp.max(top, axis=(0, 1), keepdims=True), (8, W))


def power_of(top):
    counts = [
        (top >= 2.0**k).astype(jnp.int32) for k in range(LOWEST_POWER, HIGHEST_POWER + 1)
    ]
    while len(counts) > 1:
        counts = [sum(counts[i : i + 2]) for i in range(0, len(counts), 2)]
    return counts[0] + (LOWEST_POWER - 1)


def by_power(power, sign, bits):
    steps = power - (LOWEST_POWER - 1)
    factor = jnp.full((8, W), 2.0 ** (sign * (bits - LOWEST_POWER + 1)), F32)
    for bit in range(6):
        factor = factor * jnp.where((steps & (1 << bit)) != 0, 2.0 ** (-sign * (1 << bit)), 1.0)
    return jnp.concatenate([factor] * (ROWS // 8), axis=0)


def packed(planes, power):
    factor = by_power(power, 1, 22)
    words = []
    for i in range(0, len(planes), 4):
        q = [
            jnp.minimum(jnp.floor(plane * factor + 0.5), 2.0**23 - 1).astype(jnp.int32)
            for plane in planes[i : i + 4]
        ]
        last = (q[3] & 255, (q[3] >> 8) & 255, (q[3] >> 16) & 255)
        words += [(q[k] << 8) | last[k] for k in range(3)]
    return words


def unpacked(places):
    factors = [by_power(ref[at : at + 8, :], -1, 22) for ref, _, at in places]
    held = {}

    def plane(j):
        group = j // 4
        if group not in held:
            ref, start, _ = places[j // HALF]
            at = start + (group - j // HALF * (HALF // 4)) * 3 * ROWS
            words = [ref[at + k * ROWS : at + (k + 1) * ROWS, :] for k in range(3)]
            last = ((words[2] & 255) << 24) | ((words[1] & 255) << 16) | ((words[0] & 255) << 8)
            held[group] = [
                (q >> 8).astype(F32) * factors[j // HALF] for q in (*words, last)
            ]
        return held[group][j % 4]

    return plane


def put(target, start, words):
    for k, word in enumerate(words):
        target[start + k * ROWS : start + (k + 1) * ROWS, :] = word


def coded(levels, powers=1):
    return jax.ShapeDtypeStruct((levels // 4 * 3 * ROWS + 8 * powers, W), jnp.int32)


def widened(source, target):
    def step(i, carry):
        for k in range(4):
            c = i * 4 + k
            target[pl.ds(c * PITCH, ROWS), :] = source[c].reshape(ROWS, W).astype(F32)
        return carry

    lax.fori_loop(0, C // 4, step, 0)


def turned_group(source, g):
    return [
        source[pl.ds(g * GROUP + i, C, stride=PITCH), :].astype(BF16) for i in range(GROUP)
    ]


def correlate(base, mirrored, turned_ref, partner_s, grams, horiz_s):
    row = lax.broadcasted_iota(jnp.int32, (W, W), 0)
    col = lax.broadcasted_iota(jnp.int32, (W, W), 1)
    turn = (row == jnp.where(mirrored == 1, W - 1 - col, col)).astype(BF16)
    lane = lax.broadcasted_iota(jnp.int32, (8, W), 1)
    sub = lax.broadcasted_iota(jnp.int32, (8, W), 0)
    offset = jnp.where(mirrored == 1, W - 1 - lane, lane) + base
    index = (sub + offset) & 7
    stay = sub + (offset & 7) < 8
    inside = offset < W

    def products(g):
        partner = lax.dot_general(
            turn, jnp.concatenate(turned_group(partner_s, g), axis=0), (((1,), (1,)), ((), ())),
            preferred_element_type=F32).astype(BF16)
        mine = [turned_ref[g * W + i * C : g * W + (i + 1) * C, :] for i in range(GROUP)]
        blank = jnp.zeros((C, W), BF16)
        blocks = jnp.concatenate(
            [
                jnp.concatenate([mine[i] if i == k else blank for k in range(GROUP)], axis=1)
                for i in range(GROUP)
            ],
            axis=0,
        )
        grams[g % 2][...] = jnp.dot(partner, blocks, preferred_element_type=F32)

    def shift(g):
        gram = grams[g % 2]
        for i in range(GROUP):
            tiles = [gram[8 * k : 8 * k + 8, i * W : (i + 1) * W] for k in range(W // 8)]
            tiles += [jnp.zeros((8, W), F32)] * 4
            for bit, count in ((6, 12), (5, 8), (4, 6), (3, 5)):
                step = 1 << (bit - 3)
                take = (offset & (1 << bit)) != 0
                tiles = [jnp.where(take, tiles[k + step], tiles[k]) for k in range(count)]
            tiles = [
                jnp.take_along_axis(tile, index, axis=0, mode="promise_in_bounds") for tile in tiles
            ]
            for k in range(NDISP // 8):
                value = jnp.where(inside, jnp.where(stay, tiles[k], tiles[k + 1]), 0.0)
                horiz_s[pl.ds((g * GROUP + i) * PITCH + 8 * k, 8), :] = value

    groups = ROWS // GROUP
    products(0)
    for g in range(groups):
        if g + 1 < groups:
            products(g + 1)
        shift(g)


def near_kernel(base_ref, own_hbm, near_ref, turned_ref, part_ref,
                own_ref, sem, own_s, near_s, gram_0, gram_1, horiz_s):
    fetch = pltpu.make_async_copy(own_hbm, own_ref, sem)
    fetch.start()
    widened(near_ref, near_s)
    fetch.wait()
    widened(own_ref, own_s)
    for g in range(ROWS // GROUP):
        turned_ref[g * W : (g + 1) * W, :] = jnp.concatenate(turned_group(own_s, g), axis=0)
    correlate(base_ref[0], 1 - lax.axis_index("cam") % 2, turned_ref, near_s,
              (gram_0, gram_1), horiz_s)
    for level in range(NDISP):
        part_ref[level] = horiz_s[pl.ds(level, ROWS, stride=PITCH), :]


def next_kernel(base_ref, turned_ref, next_ref, part_ref, high_ref, low_ref, code_ref,
                next_s, gram_0, gram_1, horiz_s):
    widened(next_ref, next_s)
    correlate(base_ref[0], lax.axis_index("cam") % 2, turned_ref, next_s,
              (gram_0, gram_1), horiz_s)
    for level in range(NDISP):
        summed = (part_ref[level] + horiz_s[pl.ds(level, ROWS, stride=PITCH), :]) * FACTOR
        if level < HALF:
            low_ref[level] = summed
        else:
            high_ref[level - HALF] = summed
    planes = [high_ref[k] for k in range(HALF)]
    power = power_of(largest_of(planes))
    put(code_ref, 0, packed(planes, power))
    code_ref[HALF_WORDS : HALF_WORDS + 8, :] = power


FLAT = pltpu.VMEM((C * PITCH, W), F32)
GRAM = pltpu.VMEM((W, GROUP * W), F32)


def with_near(base, own, near):
    return pl.pallas_call(
        near_kernel,
        out_shape=(jax.ShapeDtypeStruct((ROWS * C, W), BF16),
                   jax.ShapeDtypeStruct((NDISP, ROWS, W), F32)),
        in_specs=[SMEM, ANY, VMEM],
        out_specs=(VMEM, VMEM),
        scratch_shapes=[pltpu.VMEM((C, T, H, W), BF16), pltpu.SemaphoreType.DMA,
                        FLAT, FLAT, GRAM, GRAM, FLAT],
        compiler_params=pltpu.CompilerParams(vmem_limit_bytes=12 << 20),
        cost_estimate=pl.CostEstimate(flops=1 << 30, bytes_accessed=2 << 20, transcendentals=0),
        name="with_near",
    )(base, own, near)


def with_next(base, turned, following, part):
    half = jax.ShapeDtypeStruct((HALF, ROWS, W), F32)
    return pl.pallas_call(
        next_kernel,
        out_shape=(half, half, coded(HALF)),
        in_specs=[SMEM, VMEM, VMEM, VMEM],
        out_specs=(VMEM, VMEM, VMEM),
        scratch_shapes=[FLAT, GRAM, GRAM, FLAT],
        compiler_params=pltpu.CompilerParams(vmem_limit_bytes=12 << 20),
        cost_estimate=pl.CostEstimate(flops=1 << 30, bytes_accessed=2 << 20, transcendentals=0),
        name="with_next",
    )(base, turned, following, part)


def along_kernel(row_step, base_ref, own_ref, high_ref, low_ref, same_ref, other_ref,
                 cost_ref, code_ref, all_ref, pair_s, vert_s):
    base = base_ref[0]
    half = H // 2
    size = C * T * 2 * H + H
    same_at = ((lax.axis_index("cam") // row_step) % 2) * size
    other_at = size - same_at
    zeros = jnp.zeros((H, W), F32)
    for start in (0, size):
        pair_s[start : start + H, :] = zeros

    def widen(i, carry):
        for k in range(2):
            c = i * 2 + k
            for source, at in ((same_ref, same_at), (other_ref, other_at)):
                for t in range(T):
                    start = pl.multiple_of(at + (c * T + t) * 2 * H + H, H)
                    pair_s[pl.ds(start, H), :] = source[c, t].astype(F32)
                    pair_s[pl.ds(start + H, H), :] = zeros
        return carry

    lax.fori_loop(0, C // 2, widen, 0)

    for t in range(T):

        def channels(i, sums, t=t):
            for k in range(4):
                c = i * 4 + k
                mine = own_ref[c, t].astype(F32)
                mine_low, mine_high = mine[:half], mine[half:]
                start = (c * T + t) * 2 * H + H
                results = []
                for level in range(H):
                    low, high = sums[2 * level], sums[2 * level + 1]
                    part_low = pair_s[pl.ds(size + start + level, half), :]
                    part_high = pair_s[pl.ds(start + half - level, half), :]
                    if level < half:
                        part_low = part_low + pair_s[pl.ds(start - level, half), :]
                        part_high = part_high + pair_s[pl.ds(size + start + half + level, half), :]
                    results += [low + mine_low * part_low, high + mine_high * part_high]
                sums = tuple(results)
            return sums

        sums = lax.fori_loop(0, C // 4, channels,
                             tuple(jnp.zeros((half, W), F32) for _ in range(2 * H)))
        for level in range(H):
            vert_s[level, t * H : t * H + half, :] = sums[2 * level]
            vert_s[level, t * H + half : (t + 1) * H, :] = sums[2 * level + 1]
    for level in range(H, H + 4):
        vert_s[level] = jnp.zeros((ROWS, W), F32)
    for level in range(HALF):
        cost_ref[level] = low_ref[level] + vert_s[base + level] * FACTOR
    planes = [cost_ref[level] for level in range(HALF)]
    power = power_of(largest_of(planes))
    words = packed(planes, power)
    put(code_ref, 0, words)
    code_ref[HALF_WORDS : HALF_WORDS + 8, :] = power
    all_ref[0 : HALF_WORDS + 8, :] = high_ref[...]
    put(all_ref, HALF_WORDS + 8, words)
    all_ref[2 * HALF_WORDS + 8 :, :] = power


def along(row_step, base, own, high, low, same, other):
    padded = pltpu.VMEM((2 * (C * T * 2 * H + H), W), F32)
    return pl.pallas_call(
        functools.partial(along_kernel, row_step),
        out_shape=(jax.ShapeDtypeStruct((HALF, ROWS, W), F32), coded(HALF), coded(NDISP, 2)),
        in_specs=[SMEM] + [VMEM] * 5,
        out_specs=(VMEM,) * 3,
        scratch_shapes=[padded, pltpu.VMEM((H + 4, ROWS, W), F32)],
        compiler_params=pltpu.CompilerParams(vmem_limit_bytes=12 << 20),
        cost_estimate=pl.CostEstimate(flops=2 << 30, bytes_accessed=2 << 20, transcendentals=0),
        name="along",
    )(base, own, high, low, same, other)


def prepare_kernel(last, one_hbm, bias_hbm, two_hbm, one_ref, bias_ref, two_ref,
                   one_in, bias_in, two_in, sems):
    fetches = [
        pltpu.make_async_copy(source, target, sems.at[k])
        for k, (source, target) in enumerate(
            ((one_hbm, one_in), (bias_hbm, bias_in), (two_hbm, two_in)))
    ]
    for fetch in fetches:
        fetch.start()
    for fetch in fetches:
        fetch.wait()
    place = lax.axis_index("tm")
    keep_first = jnp.where(place > 0, 1.0, 0.0)
    keep_last = jnp.where(place < last, 1.0, 0.0)
    sub = lax.broadcasted_iota(jnp.int32, (ROWS, W), 0)
    lane = lax.broadcasted_iota(jnp.int32, (ROWS, W), 1)
    frame, row = sub >> 4, sub & 15

    def taps(frame_in, row_in):
        a, b = frame_in - frame, row_in - row + 1
        valid = (a >= 0) & (a <= 2) & (b >= 0) & (b <= 2)
        return jnp.where(valid, 3 * a + b, -99)

    keeps = (
        jnp.where(frame == 0, keep_first, 1.0),
        jnp.where(frame == 1, keep_last, 1.0),
    )
    tap = taps((lane & 63) >> 4, lane & 15)
    for o in range(HID):
        rows = slice(o * ROWS, (o + 1) * ROWS)
        for e in range(3):
            value = jnp.zeros((ROWS, W), F32)
            for q in range(9):
                value = jnp.where(tap == q, one_in[q // 3, q % 3, o, e], value)
            for p in range(2):
                first, second = two_parts(value * keeps[p])
                one_ref[e, p, rows, 0:W] = first
                one_ref[e, p, rows, W : 2 * W] = second
        for p in range(2):
            bias_ref[p * W + o * ROWS : p * W + (o + 1) * ROWS, :] = bias_in[o] * keeps[p]
    for p in range(2):
        tap = taps(2 * p + ((lane >> 4) & 1), lane & 15) + 9 * (lane >> 5)
        code = jnp.where(taps(2 * p + ((lane >> 4) & 1), lane & 15) < 0, -1, tap)
        for e in range(3):
            value = jnp.zeros((ROWS, W), F32)
            for q in range(9 * HID):
                value = jnp.where(code == q, two_in[(q % 9) // 3, q % 3, q // 9, e], value)
            first, second = two_parts(value)
            for copy in range(2):
                cols = slice(copy * W, (copy + 1) * W)
                two_ref[p, e * ROWS : (e + 1) * ROWS, cols] = first
                two_ref[p, (3 + e) * ROWS : (4 + e) * ROWS, cols] = second


def prepare(last, conv_one, conv_bias, conv_two):
    return pl.pallas_call(
        functools.partial(prepare_kernel, last),
        out_shape=(
            jax.ShapeDtypeStruct((3, 2, W, 2 * W), BF16),
            jax.ShapeDtypeStruct((2 * W, W), F32),
            jax.ShapeDtypeStruct((2, 6 * ROWS, 2 * W), BF16),
        ),
        in_specs=[ANY] * 3,
        out_specs=(VMEM,) * 3,
        scratch_shapes=[pltpu.SMEM((3, 3, HID, 3), F32), pltpu.SMEM((HID,), F32),
                        pltpu.SMEM((3, 3, HID, 3), F32), pltpu.SemaphoreType.DMA((3,))],
        compiler_params=pltpu.CompilerParams(vmem_limit_bytes=6 << 20),
        cost_estimate=pl.CostEstimate(flops=1 << 20, bytes_accessed=1 << 19, transcendentals=0),
        name="prepare",
    )(*(pltpu.with_memory_space_constraint(x, pltpu.HBM) for x in (
        conv_one.transpose(1, 2, 0, 3), conv_bias, conv_two.transpose(1, 2, 0, 3))))


def from_left(x):
    lane = lax.broadcasted_iota(jnp.int32, (1, W), 1)
    return jnp.where(lane == 0, 0.0, pltpu.roll(x, 1, 1))


def from_right(x):
    lane = lax.broadcasted_iota(jnp.int32, (1, W), 1)
    return jnp.where(lane == W - 1, 0.0, pltpu.roll(x, W - 1, 1))


def convolve(pair, frames, one_ref, bias_ref, two_ref, scratch, write):
    steps = NDISP // LEVELS
    spread, middle = scratch[:2], scratch[2:]

    def split(s):
        target = spread[s % 2]
        for k in range(LEVELS):
            x = jnp.concatenate([plane(s * LEVELS + k) for plane in frames], axis=0)
            for e, value in enumerate((from_left(x), x, from_right(x))):
                for q, part in enumerate(two_parts(value)):
                    target[e, q, :, k * W : (k + 1) * W] = part

    def first(s):
        source, target = spread[s % 2], middle[s % 2]
        total = None
        for e in range(3):
            parts = [source[e, q] for q in range(2)]
            term = jnp.dot(one_ref[e, pair], jnp.concatenate(parts * 2, axis=0),
                           preferred_element_type=F32)
            total = term if total is None else total + term
        bias = bias_ref[W * pair : W * pair + W, :]
        hidden = jnp.maximum(total + jnp.concatenate([bias] * LEVELS, axis=1), 0.0)
        for q, part in enumerate(two_parts(hidden)):
            target[q * W : (q + 1) * W, :] = part

    def second(s):
        total = jnp.dot(two_ref[pair], middle[s % 2][...], preferred_element_type=F32)
        both = total[: 3 * ROWS] + total[3 * ROWS :]
        for k in range(LEVELS):
            mine = both[:, k * W : (k + 1) * W]
            write(s * LEVELS + k, (
                from_left(mine[0:ROWS]) + mine[ROWS : 2 * ROWS] + from_right(mine[2 * ROWS :])))

    split(0)
    for s in range(steps + 1):
        if s + 1 < steps:
            split(s + 1)
        if s < steps:
            first(s)
        if s > 0:
            second(s - 1)


def early_kernel(low_code, high_code, low_ref, high_ref, one_ref, bias_ref, two_ref, agg_ref,
                 *scratch):
    before = unpacked(((low_code, 0, HALF_WORDS), (high_code, 0, HALF_WORDS)))

    def cost(j):
        return low_ref[j] if j < HALF else high_ref[j - HALF]

    def write(j, value):
        agg_ref[j] = cost(j) + value

    convolve(0, (before, cost), one_ref, bias_ref, two_ref, scratch, write)


def late_kernel(base_ref, code_ref, low_ref, high_ref, early_ref, one_ref, bias_ref, two_ref,
                out_ref, agg_s, *scratch):
    after = unpacked(
        ((code_ref, HALF_WORDS + 8, 2 * HALF_WORDS + 8), (code_ref, 0, HALF_WORDS)))

    def write(j, value):
        agg_s[j] = early_ref[j] + value

    def cost(j):
        return low_ref[j] if j < HALF else high_ref[j - HALF]

    convolve(1, (cost, after), one_ref, bias_ref, two_ref, scratch, write)

    base = base_ref[0].astype(F32)
    largest = agg_s[0]
    for j in range(1, NDISP):
        largest = jnp.maximum(largest, agg_s[j])
    weight = jnp.zeros((ROWS, W), F32)
    moment = jnp.zeros((ROWS, W), F32)
    for j in range(NDISP):
        e = jnp.exp(agg_s[j] - largest)
        weight = weight + e
        moment = moment + e * (base + float(j))
    out_ref[...] = moment / weight


def conv_call(kernel, out_shape, in_specs, sums, *operands):
    sums = [pltpu.VMEM((levels, ROWS, W), F32) for levels in sums]
    spread = pltpu.VMEM((3, 2, 2 * ROWS, LEVELS * W), BF16)
    middle = pltpu.VMEM((2 * W, LEVELS * W), BF16)
    return pl.pallas_call(
        kernel,
        out_shape=jax.ShapeDtypeStruct(out_shape, F32),
        in_specs=in_specs,
        out_specs=VMEM,
        scratch_shapes=sums + [spread, spread, middle, middle],
        compiler_params=pltpu.CompilerParams(vmem_limit_bytes=12 << 20),
        cost_estimate=pl.CostEstimate(
            flops=1 << 30, bytes_accessed=1 << 20, transcendentals=0),
    )(*operands)


def shards(features, disparity_base, conv_one, conv_bias, conv_two):
    own = features[0]
    cameras = lax.axis_size("cam")
    row_step = cameras // RIG_COLS
    same = swapped(own, lambda k: k ^ row_step)
    near = swapped(own, lambda k: k ^ 1)
    following = swapped(own, lambda k: (k - 1 + 2 * (k % 2)) % cameras)
    other = swapped(same, lambda k: k ^ (2 * row_step))
    turned, part = with_near(
        disparity_base, pltpu.with_memory_space_constraint(own, pltpu.HBM), near)
    cost_high, low, code_high = with_next(disparity_base, turned, following, part)
    before_high = shifted_along(code_high, "tm", 1)
    cost_low, code_low, code_all = along(
        row_step, disparity_base, own, code_high, low, same, other)
    before_low = shifted_along(code_low, "tm", 1)
    after = shifted_along(code_all, "tm", -1)
    matrices = prepare(lax.axis_size("tm") - 1, conv_one, conv_bias, conv_two)
    early = conv_call(early_kernel, (NDISP, ROWS, W), [VMEM] * 7, (),
                      before_low, before_high, cost_low, cost_high,
                      *matrices)
    out = conv_call(late_kernel, (ROWS, W), [SMEM] + [VMEM] * 7, (NDISP,),
                    disparity_base, after, cost_low, cost_high, early,
                    *matrices)
    return out.reshape(1, T, H, W)


def solution(mesh):
    in_specs = (P("cam", None, "tm", None, None), P(), P(), P(), P())
    out_specs = P("cam", "tm", None, None)
    return jax.shard_map(shards, mesh=mesh, in_specs=in_specs, out_specs=out_specs, check_vma=False)
```
